32 devices in a mesh: groups: 2 (over x), ctx: 16 (over z, y, core).
Axes of the slice: x: 2, y: 2, z: 4, core: 2. Of those that a mesh axis runs over, the one named last changes fastest.
Arguments:
- queries: bfloat16 [8192, 1024], P(('groups', 'ctx')), parts along dimension 0, may hold values from -128 to 128
- keys: bfloat16 [8192, 128], P(('groups', 'ctx')), parts along dimension 0, may hold values from -32 to 32
- values: bfloat16 [8192, 128], P(('groups', 'ctx')), parts along dimension 0, may hold values from -6 to 6
- doc_ids: int32 [8192], P(('groups', 'ctx')), parts along dimension 0, may hold values from 0 to 2, never falling along the last dimension, each value on 1 to 3072 neighbouring positions
Outputs:
- attended: bfloat16 [8192, 1024], P(('groups', 'ctx')), parts along dimension 0
The draws below stay inside these ranges and needn't reach their ends.
There are 2 independent parts, one for each index of `groups`. The reference program is written for one: setup_inputs(seed, part) draws one part's arguments, and reference() takes and returns one part's arrays. A program takes and returns all parts, laid end to end along the dimension named above; each array names one. Nothing has to cross between parts.
All inputs are finite; a program needn't handle non-finite values.
Results may differ from the reference program's by a relative error of at most 0.0041.
Values may be sent and summed in bfloat16 or wider, within the bound.
A program may use at most 64 MiB of HBM per device.

```python
import math
import jax
import jax.numpy as jnp
import numpy as np
from jax import lax

HEADS = 8
HEAD_DIM = 128
DOCS = 3
HALF = 128
SEQ = 4096
LONGEST = 3072


def drawn_pair(key):
    base = jax.random.fold_in(key, 7)
    key_one, key_two = jax.random.split(base, 2)
    keys = jnp.clip(jax.random.normal(key_one, (SEQ, HEAD_DIM), jnp.float32), -6.0, 6.0)
    queries = jnp.clip(jax.random.normal(key_two, (SEQ, HEADS * HEAD_DIM), jnp.float32), -6.0, 6.0)
    return (queries, keys)


def draw_queries(key, part):
    return drawn_pair(key)[0].astype(jnp.bfloat16)


def draw_keys(key, part):
    return drawn_pair(key)[1].astype(jnp.bfloat16)


def level_of(stream_key, dims, cuts, smallest, top_value):
    gain = 1.0
    for dim, parts in cuts:
        heights = jax.random.uniform(jax.random.fold_in(jax.random.fold_in(stream_key, 6), dim), (parts,), jnp.float32, smallest / len(cuts), top_value / len(cuts))
        gain = gain * jnp.repeat(jnp.exp(heights), dims[dim] // parts).reshape((-1,) + (1,) * (len(dims) - 1 - dim))
    return gain


def profile(number_of, total, limit, lean):
    portions = [(1 << 20) // math.isqrt(grade ** lean) + 1 for grade in range(2, number_of + 1)]
    rest, counts = total - limit - (number_of - 1), [1] * (number_of - 1)
    while rest > 0:
        candidates = [i for i in range(number_of - 1) if counts[i] < limit]
        pool, left = sum([portions[i] for i in candidates]), rest
        for i in candidates:
            extra = min(limit - counts[i], max(1, left * portions[i] // pool), rest)
            counts[i] = counts[i] + extra
            rest = rest - extra
    return np.array([limit] + counts)


def ragged_sizes(rng, amount, total, bound, lean):
    if amount == 2:
        one = jax.random.randint(rng, (), max(1, total - bound), min(bound, total - 1) + 1)
        return jnp.stack([one, total - one])
    sizes = jnp.asarray(profile(amount, total, bound, lean), jnp.int32)
    couples = (amount - 1) // 2
    giver, receiver = sizes[1:1 + 2 * couples:2], sizes[2:2 + 2 * couples:2]
    slack = jnp.minimum(giver - 1, bound - receiver)
    passed = jax.random.randint(jax.random.fold_in(rng, 1), (couples,), 0, 1 << 20) % (slack + 1)
    sizes = sizes.at[1:1 + 2 * couples:2].set(giver - passed).at[2:2 + 2 * couples:2].set(receiver + passed)
    return sizes[jax.random.permutation(jax.random.fold_in(rng, 2), amount)]


def centred(key, dims, deviation, reach, cuts=(), kind=jnp.bfloat16):
    values = deviation * jax.random.normal(key, dims, jnp.float32)
    if cuts:
        values = values * level_of(key, dims, cuts, -0.22, 0.18)
    return jnp.clip(values, -reach, reach).astype(kind)


def setup_inputs(seed: int = 0, part: int = 0) -> dict:
    splits = jax.random.split(jax.random.key(seed), 5)
    part_splits = jax.random.split(jax.random.fold_in(splits[4], part), 5)
    return {
        "queries": draw_queries(jax.random.fold_in(jax.random.fold_in(splits[4], part), 71), part),
        "keys": draw_keys(jax.random.fold_in(jax.random.fold_in(splits[4], part), 71), part),
        "values": centred(part_splits[2], (SEQ, HEAD_DIM), 1.0, 6.0, ((0, 16),)),
        "doc_ids": jnp.searchsorted(jnp.cumsum(ragged_sizes(part_splits[3], DOCS, SEQ, LONGEST, 0)), jnp.arange(SEQ), side="right").astype(jnp.int32),
    }


def reference(queries, keys, values, doc_ids):
    score_scale = HEAD_DIM ** -0.5
    positions = jnp.arange(SEQ, dtype=jnp.int32)

    def query_block(block_index):
        start_row = (block_index * HALF).astype(jnp.int32)
        query_rows = lax.dynamic_slice_in_dim(queries, start_row, HALF, 0).reshape(HALF * HEADS, HEAD_DIM)
        scores = jnp.dot(query_rows, keys.T, preferred_element_type=jnp.float32) * score_scale
        query_place = jnp.repeat(start_row + jnp.arange(HALF, dtype=jnp.int32), HEADS)
        query_doc = jnp.repeat(lax.dynamic_slice_in_dim(doc_ids, start_row, HALF, 0), HEADS)
        visible = (positions[None, :] <= query_place[:, None]) & (doc_ids[None, :] == query_doc[:, None])
        row_max = jnp.max(jnp.where(visible, scores, -jnp.inf), axis=1)
        weights = jnp.where(visible, jnp.exp(scores - row_max[:, None]), 0.0)
        row_sum = jnp.sum(weights, axis=1)
        result = jnp.dot(weights.astype(jnp.bfloat16), values, preferred_element_type=jnp.float32) / row_sum[:, None]
        return result.astype(jnp.bfloat16).reshape(HALF, HEADS * HEAD_DIM)

    blocks = lax.map(query_block, jnp.arange(SEQ // HALF, dtype=jnp.int32))
    return blocks.reshape(SEQ, HEADS * HEAD_DIM)
```

```python
import functools

import jax
import jax.numpy as jnp
from jax import lax
from jax.experimental import pallas as pl
from jax.experimental.pallas import tpu as pltpu
from jax.sharding import PartitionSpec as P

HIDDEN = -1e30
LOG2E = 1.4426950408889634
DOCS = 3
TILE_HEADS = 2


def kernel(
    n,
    q_hbm,
    k_hbm,
    v_hbm,
    d_hbm,
    o_ref,
    q_ref,
    kv,
    docs,
    m_ref,
    acc_ref,
    qs,
    fill_sem,
    send_kv,
    recv_kv,
    send_doc,
    recv_doc,
):
    rows, width = q_hbm.shape
    dim = k_hbm.shape[1]
    heads = width // dim
    levels = n // 4
    window = 3 * n // 4
    depth = (window + 3) // 4
    me = lax.axis_index("ctx")
    z = me // 4
    r = me % 4
    y = r // 2
    c = r % 2
    chip = me // 2
    up = me + 4
    across = z * 4 + (1 - y) * 2 + c
    partner = z * 4 + y * 2 + (1 - c)
    scale = dim ** (-0.5) * LOG2E
    top = z == levels - 1
    last = jnp.minimum(z, depth)

    barrier = pltpu.get_barrier_semaphore()

    def greet(device):
        pl.semaphore_signal(
            barrier, inc=1, device_id={"ctx": device}, device_id_type=pl.DeviceIdType.MESH
        )

    @pl.when(z > 0)
    def _():
        greet(me - 4)

    @pl.when(z < levels - 1)
    def _():
        greet(up)

    greet(across)
    greet(partner)

    def span(block):
        return pl.ds(pl.multiple_of(block * rows, rows), rows)

    fills = [
        pltpu.make_async_copy(k_hbm, kv.at[0, span(me), :], fill_sem.at[0]),
        pltpu.make_async_copy(v_hbm, kv.at[1, span(me), :], fill_sem.at[1]),
        pltpu.make_async_copy(d_hbm, docs.at[me], fill_sem.at[2]),
    ]
    for fill in fills:
        fill.start()
    query_fill = pltpu.make_async_copy(q_hbm, q_ref, fill_sem.at[3])
    query_fill.start()

    def copies(stream, lands, level, piece, block, device):
        made = [
            pltpu.make_async_remote_copy(
                src_ref=kv.at[piece, span(block), :],
                dst_ref=kv.at[piece, span(block), :],
                send_sem=send_kv.at[stream, level, piece],
                recv_sem=recv_kv.at[lands, level, piece],
                device_id={"ctx": device},
                device_id_type=pl.DeviceIdType.MESH,
            )
        ]
        if piece == 0:
            made.append(
                pltpu.make_async_remote_copy(
                    src_ref=docs.at[block],
                    dst_ref=docs.at[block],
                    send_sem=send_doc.at[stream, level],
                    recv_sem=recv_doc.at[lands, level],
                    device_id={"ctx": device},
                    device_id_type=pl.DeviceIdType.MESH,
                )
            )
        return made

    def start(stream, lands, *where):
        for copy in copies(stream, lands, *where):
            copy.start()

    def arrived(lands, *where):
        for copy in copies(lands, lands, *where):
            copy.wait_recv()

    def sent(stream, lands, *where):
        for copy in copies(stream, lands, *where):
            copy.wait_send()

    def needs(some_chip, chunk):
        return (chunk <= some_chip) & (2 * chunk + 1 >= 2 * some_chip - window)

    def from_under(some_z, some_y, level):
        return (some_y == 0) & (some_z - level == depth) & needs(2 * some_z, 2 * level + 1)

    def climbs(level):
        return (z < levels - 1) & (z - level < depth)

    def crosses(level):
        return needs(2 * z + 1 - y, 2 * level + y) & jnp.logical_not(from_under(z, 1 - y, level))

    def crossed(level):
        return needs(chip, 2 * level + 1 - y)

    def passes(level):
        return (z < levels - 1) & from_under(z + 1, y, level)

    def own(level):
        return level * 4 + r

    def other(level):
        return level * 4 + 2 * (1 - y) + c

    def relay(level, piece):
        @pl.when(climbs(level))
        def _():
            start(0, 0, level, piece, own(level), up)

        @pl.when(crosses(level))
        def _():
            start(1, 1, level, piece, own(level), across)

        start(2, 2, level, piece, own(level), partner)

    def from_below(level):
        for piece in range(2):
            arrived(0, level, piece, own(level), up)
            relay(level, piece)

    def from_across(level):
        @pl.when(crossed(level))
        def _():
            for piece in range(2):
                arrived(1, level, piece, other(level), across)

                @pl.when(passes(level))
                def _():
                    start(4, 1, level, piece, other(level), up)

                start(3, 3, level, piece, other(level), partner)

    def own_pair(level):
        for piece in range(2):
            arrived(2, level, piece, level * 4 + 2 * y + 1 - c, partner)

    def other_pair(level):
        @pl.when(crossed(level))
        def _():
            for piece in range(2):
                arrived(3, level, piece, level * 4 + 2 * (1 - y) + 1 - c, partner)

    def finish(level):
        for piece in range(2):

            @pl.when(climbs(level))
            def _():
                sent(0, 0, level, piece, own(level), up)

            @pl.when(crosses(level))
            def _():
                sent(1, 1, level, piece, own(level), across)

            sent(2, 2, level, piece, own(level), partner)

            @pl.when(crossed(level))
            def _():
                sent(3, 3, level, piece, other(level), partner)

                @pl.when(passes(level))
                def _():
                    sent(4, 1, level, piece, other(level), up)

    pl.semaphore_wait(barrier, 2 + jnp.minimum(z, 1) + jnp.minimum(levels - 1 - z, 1))
    for fill in fills[:1] + fills[2:]:
        fill.wait()
    relay(z, 0)
    fills[1].wait()
    relay(z, 1)

    lane = lax.broadcasted_iota(jnp.int32, (rows, dim), 1)
    row = lax.broadcasted_iota(jnp.int32, (rows, dim), 0)

    def doc_of(block):
        ids = docs[block]
        number = jnp.zeros((rows, dim), jnp.int32)
        for doc in range(1, DOCS):
            under = jnp.sum(jnp.where(ids < doc, 1.0, 0.0), axis=1, keepdims=True).astype(jnp.int32)
            number = number + jnp.where(row >= under, 1, 0)
        return number

    query_marks = jnp.where(lane == doc_of(me), 0.0, HIDDEN).astype(jnp.bfloat16)
    query_fill.wait()
    for head in range(heads):
        here = slice(head * rows, (head + 1) * rows)
        qs[here, :dim] = q_ref[:, head * dim : (head + 1) * dim]
        qs[here, dim:] = query_marks

    tile_rows = TILE_HEADS * rows
    tiles = heads // TILE_HEADS

    def attend(block, first=False):
        place = span(block)
        marks = jnp.where(lane == doc_of(block), 1.0, 0.0).astype(jnp.bfloat16)
        k_block = jnp.concatenate([kv[0, place, :], marks], axis=1)
        v_block = jnp.concatenate([kv[1, place, :], jnp.ones((rows, dim), jnp.bfloat16)], axis=1)

        def scores(tile):
            return lax.dot_general(
                qs[tile * tile_rows : (tile + 1) * tile_rows, :],
                k_block,
                (((1,), (1,)), ((), ())),
                preferred_element_type=jnp.float32,
            )

        following = scores(0)
        for tile in range(tiles):
            s = following
            if tile + 1 < tiles:
                following = scores(tile + 1)
            here = slice(tile * tile_rows, (tile + 1) * tile_rows)
            if first:
                key_id = lax.broadcasted_iota(jnp.int32, (rows, rows), 1)
                query_id = lax.broadcasted_iota(jnp.int32, (rows, rows), 0)
                hide = jnp.where(key_id <= query_id, 0.0, HIDDEN)
                s = s + jnp.concatenate([hide] * TILE_HEADS, axis=0)
            new = jnp.broadcast_to(jnp.max(s, axis=1, keepdims=True), (tile_rows, dim))
            if not first:
                old = m_ref[here]
                new = jnp.maximum(old, new)
            m_ref[here] = new
            w = jnp.exp2((s - jnp.tile(new, (1, rows // dim))) * scale)
            part = jnp.dot(w.astype(jnp.bfloat16), v_block, preferred_element_type=jnp.float32)
            if first:
                acc_ref[here] = part
            else:
                acc_ref[here] = (
                    acc_ref[here] * jnp.tile(jnp.exp2((old - new) * scale), (1, 2)) + part
                )

    def process(block):
        @pl.when((block <= me) & (block >= me - window))
        def _():
            attend(block)

    attend(me, True)
    own_pair(z)
    process(me + 1 - 2 * c)

    @pl.when(jnp.logical_not(top))
    def _():
        def ahead(i, carry):
            from_below(z - i)
            return carry

        lax.fori_loop(1, last + 1, ahead, 0)

    def step(i, carry):
        level = z - i

        @pl.when(top)
        def _():
            from_below(level)

        process(level * 4 + r)
        from_across(level + 1)
        process((level + 1) * 4 + 2 * (1 - y) + c)
        own_pair(level)
        process(level * 4 + 2 * y + 1 - c)
        other_pair(level + 1)
        process((level + 1) * 4 + 2 * (1 - y) + 1 - c)
        return carry

    lax.fori_loop(1, last + 1, step, 0)
    from_across(z - last)
    process((z - last) * 4 + 2 * (1 - y) + c)
    other_pair(z - last)
    process((z - last) * 4 + 2 * (1 - y) + 1 - c)

    for head in range(heads):
        here = slice(head * rows, (head + 1) * rows)
        o_ref[:, head * dim : (head + 1) * dim] = (acc_ref[here, :dim] / acc_ref[here, dim:]).astype(
            o_ref.dtype
        )

    def drain(i, carry):
        finish(z - i)
        return carry

    lax.fori_loop(0, last + 1, drain, 0)


def solution(mesh):
    n = mesh.shape["ctx"]

    def on_device(queries, keys, values, doc_ids):
        rows, width = queries.shape
        dim = keys.shape[1]
        heads = width // dim
        levels = n // 4
        anywhere = pl.BlockSpec(memory_space=pl.ANY)
        return pl.pallas_call(
            functools.partial(kernel, n),
            out_shape=jax.ShapeDtypeStruct((rows, width), jnp.bfloat16),
            in_specs=[anywhere] * 4,
            out_specs=pl.BlockSpec(memory_space=pltpu.VMEM),
            scratch_shapes=[
                pltpu.VMEM((rows, width), jnp.bfloat16),
                pltpu.VMEM((2, n * rows, dim), jnp.bfloat16),
                pltpu.VMEM((n, 1, rows), jnp.int32),
                pltpu.VMEM((heads * rows, dim), jnp.float32),
                pltpu.VMEM((heads * rows, 2 * dim), jnp.float32),
                pltpu.VMEM((heads * rows, 2 * dim), jnp.bfloat16),
                pltpu.SemaphoreType.DMA((4,)),
                pltpu.SemaphoreType.DMA((5, levels, 2)),
                pltpu.SemaphoreType.DMA((4, levels, 2)),
                pltpu.SemaphoreType.DMA((5, levels)),
                pltpu.SemaphoreType.DMA((4, levels)),
            ],
            compiler_params=pltpu.CompilerParams(collective_id=0, has_side_effects=True, vmem_limit_bytes=16 * 1024 * 1024),
        )(*[pltpu.with_memory_space_constraint(a, pltpu.HBM) for a in (queries, keys, values, doc_ids.reshape(1, rows))])

    spec = P(("groups", "ctx"), None)
    return jax.shard_map(
        on_device,
        mesh=mesh,
        in_specs=(spec, spec, spec, P(("groups", "ctx"))),
        out_specs=spec,
        check_vma=False,
    )
```

```python
import functools

import jax
import jax.numpy as jnp
from jax import lax
from jax.experimental import pallas as pl
from jax.experimental.pallas import tpu as pltpu
from jax.sharding import PartitionSpec as P

HIDDEN = -1e30
LOG2E = 1.4426950408889634
DOCS = 3
TILE_HEADS = 2


def kernel(
    n,
    q_hbm,
    k_hbm,
    v_hbm,
    d_hbm,
    o_ref,
    q_ref,
    kv,
    docs,
    m_ref,
    acc_ref,
    qs,
    fill_sem,
    send_kv,
    recv_kv,
    send_doc,
    recv_doc,
    ready_sem,
):
    rows, width = q_hbm.shape
    dim = k_hbm.shape[1]
    heads = width // dim
    levels = n // 4
    window = 3 * n // 4
    depth = (window + 3) // 4
    me = lax.axis_index("ctx")
    z = me // 4
    r = me % 4
    y = r // 2
    c = r % 2
    chip = me // 2
    up = me + 4
    across = z * 4 + (1 - y) * 2 + c
    partner = z * 4 + y * 2 + (1 - c)
    scale = dim ** (-0.5) * LOG2E
    top = z == levels - 1
    last = jnp.minimum(z, depth)
    quick = levels == 4
    source = (z == 1) & (y == 1) if quick else False
    aside = (z == 2) & (y == 0) if quick else False
    beyond = (z == 3) & (y == 1) if quick else False

    barrier = pltpu.get_barrier_semaphore()

    def greet(device):
        pl.semaphore_signal(
            barrier, inc=1, device_id={"ctx": device}, device_id_type=pl.DeviceIdType.MESH
        )

    @pl.when(z > 0)
    def _():
        greet(me - 4)

    @pl.when(z < levels - 1)
    def _():
        greet(up)

    greet(across)
    greet(partner)
    if quick:

        @pl.when(aside)
        def _():
            greet(me - 2)

        @pl.when(source)
        def _():
            greet(me + 8)

    def span(block):
        return pl.ds(pl.multiple_of(block * rows, rows), rows)

    fills = [
        pltpu.make_async_copy(k_hbm, kv.at[0, span(me), :], fill_sem.at[0]),
        pltpu.make_async_copy(v_hbm, kv.at[1, span(me), :], fill_sem.at[1]),
        pltpu.make_async_copy(d_hbm, docs.at[me], fill_sem.at[2]),
    ]
    for fill in fills:
        fill.start()
    query_fill = pltpu.make_async_copy(q_hbm, q_ref, fill_sem.at[3])
    query_fill.start()

    def copies(stream, lands, level, piece, block, device):
        made = [
            pltpu.make_async_remote_copy(
                src_ref=kv.at[piece, span(block), :],
                dst_ref=kv.at[piece, span(block), :],
                send_sem=send_kv.at[stream, level, piece],
                recv_sem=recv_kv.at[lands, level, piece],
                device_id={"ctx": device},
                device_id_type=pl.DeviceIdType.MESH,
            )
        ]
        if piece == 0:
            made.append(
                pltpu.make_async_remote_copy(
                    src_ref=docs.at[block],
                    dst_ref=docs.at[block],
                    send_sem=send_doc.at[stream, level],
                    recv_sem=recv_doc.at[lands, level],
                    device_id={"ctx": device},
                    device_id_type=pl.DeviceIdType.MESH,
                )
            )
        return made

    def start(stream, lands, *where):
        for copy in copies(stream, lands, *where):
            copy.start()

    def arrived(lands, *where):
        for copy in copies(lands, lands, *where):
            copy.wait_recv()

    def sent(stream, lands, *where):
        for copy in copies(stream, lands, *where):
            copy.wait_send()

    def needs(some_chip, chunk):
        return (chunk <= some_chip) & (2 * chunk + 1 >= 2 * some_chip - window)

    def from_under(some_z, some_y, level):
        return (some_y == 0) & (some_z - level == depth) & needs(2 * some_z, 2 * level + 1)

    def spared(level):
        return (z == 2) & (y == 1) & (level == 0) if quick else False

    def climbs(level):
        return (z < levels - 1) & (z - level < depth) & jnp.logical_not(spared(level))

    def crosses(level):
        direct = needs(2 * z + 1 - y, 2 * level + y) & jnp.logical_not(from_under(z, 1 - y, level))
        return direct & jnp.logical_not(spared(level))

    def crossed(level):
        return needs(chip, 2 * level + 1 - y)

    def passes(level):
        return (z < levels - 1) & from_under(z + 1, y, level)

    def own(level):
        return level * 4 + r

    def other(level):
        return level * 4 + 2 * (1 - y) + c

    def relay(level, piece):
        @pl.when(climbs(level))
        def _():
            start(0, 0, level, piece, own(level), up)

        @pl.when(crosses(level))
        def _():
            start(1, 1, level, piece, own(level), across)

        start(2, 2, level, piece, own(level), partner)

    def from_below(level):
        def plain():
            for piece in range(2):
                arrived(0, level, piece, own(level), up)
                relay(level, piece)

        if not quick:
            plain()
            return
        pl.when(jnp.logical_not(source))(plain)

        @pl.when(source)
        def _():
            for piece in range(2):
                arrived(0, level, piece, own(level), up)
                start(4, 1, level, piece, own(level), me + 2)
                start(1, 1, level, piece, own(level), across)
                start(2, 2, level, piece, own(level), partner)
            for piece in range(2):
                start(0, 0, level, piece, own(level), up)
            pl.semaphore_wait(ready_sem, 1)
            for piece in range(2):
                start(5, 0, level, piece, own(level), me + 8)

    def from_across(level):
        @pl.when(crossed(level))
        def _():
            for piece in range(2):
                arrived(1, level, piece, other(level), across)

                @pl.when(passes(level))
                def _():
                    start(4, 1, level, piece, other(level), up)

                start(3, 3, level, piece, other(level), partner)

    def own_pair(level):
        for piece in range(2):
            arrived(2, level, piece, level * 4 + 2 * y + 1 - c, partner)

    def other_pair(level):
        @pl.when(crossed(level))
        def _():
            for piece in range(2):
                arrived(3, level, piece, level * 4 + 2 * (1 - y) + 1 - c, partner)

    def finish(level):
        for piece in range(2):

            @pl.when(climbs(level))
            def _():
                sent(0, 0, level, piece, own(level), up)

            @pl.when(crosses(level))
            def _():
                sent(1, 1, level, piece, own(level), across)

            sent(2, 2, level, piece, own(level), partner)
            if quick:

                @pl.when(source & (level == 0))
                def _():
                    sent(4, 1, level, piece, own(level), me + 2)
                    sent(5, 0, level, piece, own(level), me + 8)

            @pl.when(crossed(level))
            def _():
                sent(3, 3, level, piece, other(level), partner)

                @pl.when(passes(level))
                def _():
                    sent(4, 1, level, piece, other(level), up)

    greeters = 2 + jnp.minimum(z, 1) + jnp.minimum(levels - 1 - z, 1)
    if quick:
        greeters = greeters + jnp.where(source | beyond, 1, 0)
    pl.semaphore_wait(barrier, greeters)
    if quick:

        @pl.when(beyond)
        def _():
            pl.semaphore_signal(
                ready_sem, inc=1, device_id={"ctx": me - 8}, device_id_type=pl.DeviceIdType.MESH
            )

    for fill in fills[:1] + fills[2:]:
        fill.wait()
    relay(z, 0)
    fills[1].wait()
    relay(z, 1)

    lane = lax.broadcasted_iota(jnp.int32, (rows, dim), 1)
    row = lax.broadcasted_iota(jnp.int32, (rows, dim), 0)

    def doc_of(block):
        ids = docs[block]
        number = jnp.zeros((rows, dim), jnp.int32)
        for doc in range(1, DOCS):
            under = jnp.sum(jnp.where(ids < doc, 1.0, 0.0), axis=1, keepdims=True).astype(jnp.int32)
            number = number + jnp.where(row >= under, 1, 0)
        return number

    query_marks = jnp.where(lane == doc_of(me), 0.0, HIDDEN).astype(jnp.bfloat16)
    query_fill.wait()
    for head in range(heads):
        here = slice(head * rows, (head + 1) * rows)
        qs[here, :dim] = q_ref[:, head * dim : (head + 1) * dim]
        qs[here, dim:] = query_marks

    tile_rows = TILE_HEADS * rows
    tiles = heads // TILE_HEADS

    def attend(blocks, first=False):
        ks, vs = [], []
        for block in blocks:
            place = span(block)
            marks = jnp.where(lane == doc_of(block), 1.0, 0.0).astype(jnp.bfloat16)
            ks.append(jnp.concatenate([kv[0, place, :], marks], axis=1))
            vs.append(jnp.concatenate([kv[1, place, :], jnp.ones((rows, dim), jnp.bfloat16)], axis=1))
        k_block = jnp.concatenate(ks, axis=0)
        v_block = jnp.concatenate(vs, axis=0)
        length = k_block.shape[0]

        def scores(tile):
            return lax.dot_general(
                qs[tile * tile_rows : (tile + 1) * tile_rows, :],
                k_block,
                (((1,), (1,)), ((), ())),
                preferred_element_type=jnp.float32,
            )

        following = scores(0)
        for tile in range(tiles):
            s = following
            if tile + 1 < tiles:
                following = scores(tile + 1)
            here = slice(tile * tile_rows, (tile + 1) * tile_rows)
            if first:
                key_id = lax.broadcasted_iota(jnp.int32, (rows, rows), 1)
                query_id = lax.broadcasted_iota(jnp.int32, (rows, rows), 0)
                hide = jnp.where(key_id <= query_id, 0.0, HIDDEN)
                s = s + jnp.concatenate([hide] * TILE_HEADS, axis=0)
            new = jnp.broadcast_to(jnp.max(s, axis=1, keepdims=True), (tile_rows, dim))
            if not first:
                old = m_ref[here]
                new = jnp.maximum(old, new)
            m_ref[here] = new
            w = jnp.exp2((s - jnp.tile(new, (1, length // dim))) * scale)
            part = jnp.dot(w.astype(jnp.bfloat16), v_block, preferred_element_type=jnp.float32)
            if first:
                acc_ref[here] = part
            else:
                acc_ref[here] = (
                    acc_ref[here] * jnp.tile(jnp.exp2((old - new) * scale), (1, 2)) + part
                )

    def process(chunk):
        @pl.when((chunk <= chip) & (2 * chunk + 1 >= me - window))
        def _():
            attend([2 * chunk, 2 * chunk + 1])

    attend([me], True)
    own_pair(z)

    @pl.when(c == 1)
    def _():
        attend([me - 1])

    def early(level):
        return jnp.logical_not(top) & (climbs(level) | crosses(level))

    def ahead(i, carry):
        pl.when(early(z - i))(lambda: from_below(z - i))
        return carry

    lax.fori_loop(1, last + 1, ahead, 0)

    for i in range(1, depth + 1):

        @pl.when(z >= i)
        def _():
            level = z - i
            final = (z == i) | (i == depth)
            late = final & (y == 1)
            before = jnp.logical_not(late)
            hooked = top & before if i > 1 else False
            waits = jnp.logical_not(early(level) | hooked)

            def own_set():
                pl.when(waits)(lambda: from_below(level))
                own_pair(level)

            from_across(level + 1)
            pl.when(final & jnp.logical_not(top))(lambda: from_across(level))
            pl.when(before)(own_set)
            pl.when(late)(lambda: other_pair(level + 1))
            ours, theirs = 2 * level + y, 2 * (level + 1) + 1 - y
            process(jnp.where(late, theirs, ours))
            if i < depth:
                soon = (z == i + 1) | (i + 1 == depth)
                pl.when(top & jnp.logical_not(final) & jnp.logical_not(soon & (y == 1)))(
                    lambda: from_below(level - 1)
                )
            pl.when(final & top)(lambda: from_across(level))
            pl.when(late)(own_set)
            pl.when(before)(lambda: other_pair(level + 1))
            process(jnp.where(late, ours, theirs))

    pl.when(z == 0)(lambda: from_across(z))
    other_pair(z - last)
    process(2 * (z - last) + 1 - y)

    for head in range(heads):
        here = slice(head * rows, (head + 1) * rows)
        o_ref[:, head * dim : (head + 1) * dim] = (acc_ref[here, :dim] / acc_ref[here, dim:]).astype(
            o_ref.dtype
        )

    def drain(i, carry):
        finish(z - i)
        return carry

    lax.fori_loop(0, last + 1, drain, 0)


def solution(mesh):
    n = mesh.shape["ctx"]

    def on_device(queries, keys, values, doc_ids):
        rows, width = queries.shape
        dim = keys.shape[1]
        heads = width // dim
        levels = n // 4
        anywhere = pl.BlockSpec(memory_space=pl.ANY)
        return pl.pallas_call(
            functools.partial(kernel, n),
            out_shape=jax.ShapeDtypeStruct((rows, width), jnp.bfloat16),
            in_specs=[anywhere] * 4,
            out_specs=pl.BlockSpec(memory_space=pltpu.VMEM),
            scratch_shapes=[
                pltpu.VMEM((rows, width), jnp.bfloat16),
                pltpu.VMEM((2, n * rows, dim), jnp.bfloat16),
                pltpu.VMEM((n, 1, rows), jnp.int32),
                pltpu.VMEM((heads * rows, dim), jnp.float32),
                pltpu.VMEM((heads * rows, 2 * dim), jnp.float32),
                pltpu.VMEM((heads * rows, 2 * dim), jnp.bfloat16),
                pltpu.SemaphoreType.DMA((4,)),
                pltpu.SemaphoreType.DMA((6, levels, 2)),
                pltpu.SemaphoreType.DMA((4, levels, 2)),
                pltpu.SemaphoreType.DMA((6, levels)),
                pltpu.SemaphoreType.DMA((4, levels)),
                pltpu.SemaphoreType.REGULAR,
            ],
            compiler_params=pltpu.CompilerParams(collective_id=0, has_side_effects=True, vmem_limit_bytes=16 * 1024 * 1024),
        )(*[pltpu.with_memory_space_constraint(a, pltpu.HBM) for a in (queries, keys, values, doc_ids.reshape(1, rows))])

    spec = P(("groups", "ctx"), None)
    return jax.shard_map(
        on_device,
        mesh=mesh,
        in_specs=(spec, spec, spec, P(("groups", "ctx"))),
        out_specs=spec,
        check_vma=False,
    )
```

```python
import functools

import jax
import jax.numpy as jnp
from jax import lax
from jax.experimental import pallas as pl
from jax.experimental.pallas import tpu as pltpu
from jax.sharding import PartitionSpec as P

HIDDEN = -1e30
LOG2E = 1.4426950408889634
DOCS = 3
DOC_ROWS = 16
PIECES = 4
TILE_HEADS = 2


def kernel(
    n,
    q_hbm,
    k_hbm,
    v_hbm,
    d_hbm,
    o_ref,
    q_ref,
    kv,
    docs,
    m_ref,
    acc_ref,
    qs,
    fill_sem,
    send_kv,
    recv_kv,
    recv_pair,
    send_far,
    ready_sem,
):
    rows, width = q_hbm.shape
    dim = k_hbm.shape[1]
    heads = width // dim
    levels = n // 4
    window = 3 * n // 4
    depth = (window + 3) // 4
    me = lax.axis_index("ctx")
    z = me // 4
    r = me % 4
    y = r // 2
    c = r % 2
    chip = me // 2
    up = me + 4
    across = z * 4 + (1 - y) * 2 + c
    partner = z * 4 + y * 2 + (1 - c)
    scale = dim ** (-0.5) * LOG2E
    top = z == levels - 1
    tail = top & (z >= depth)
    last = jnp.minimum(z, depth)
    quick = levels == 4
    source = (z == 1) & (y == 1) if quick else False
    aside = (z == 2) & (y == 0) if quick else False
    beyond = (z == 3) & (y == 1) if quick else False

    barrier = pltpu.get_barrier_semaphore()

    def greet(device):
        pl.semaphore_signal(
            barrier, inc=1, device_id={"ctx": device}, device_id_type=pl.DeviceIdType.MESH
        )

    @pl.when(z > 0)
    def _():
        greet(me - 4)

    @pl.when(z < levels - 1)
    def _():
        greet(up)

    greet(across)
    greet(partner)
    if quick:

        @pl.when(aside)
        def _():
            greet(me - 2)

        @pl.when(source)
        def _():
            greet(me + 8)

    assert rows <= 256 and rows % dim == 0
    stride = 2 * rows + DOC_ROWS
    half = rows // 2
    pieces = [(0, half), (half, half + DOC_ROWS), (rows + DOC_ROWS, half), (rows + DOC_ROWS + half, half)]

    def span(block, first=0, count=stride):
        return pl.ds(pl.multiple_of(block * stride + first, DOC_ROWS), count)

    doc_fill = pltpu.make_async_copy(d_hbm, docs, fill_sem.at[2])
    doc_fill.start()
    fills = [
        pltpu.make_async_copy(k_hbm, kv.at[span(me, 0, rows), :], fill_sem.at[0]),
        pltpu.make_async_copy(v_hbm, kv.at[span(me, rows + DOC_ROWS, rows), :], fill_sem.at[1]),
    ]
    for fill in fills:
        fill.start()
    query_fill = pltpu.make_async_copy(q_hbm, q_ref, fill_sem.at[3])
    query_fill.start()

    def landing(lands, level, piece):
        return recv_kv.at[lands, level, piece] if lands < 2 else recv_pair.at[lands - 2, level]

    def copy_of(stream, lands, level, piece, block, device):
        place = span(block) if piece is None else span(block, *pieces[piece])
        return pltpu.make_async_remote_copy(
            src_ref=kv.at[place, :],
            dst_ref=kv.at[place, :],
            send_sem=send_kv.at[stream, level] if stream < 4 else send_far.at[stream - 4],
            recv_sem=landing(lands, level, piece),
            device_id={"ctx": device},
            device_id_type=pl.DeviceIdType.MESH,
        )

    def start(stream, lands, level, piece, block, device):
        copy_of(stream, lands, level, piece, block, device).start()

    def arrived(lands, level, piece, block, device):
        copy_of(lands, lands, level, piece, block, device).wait_recv()

    def sent(stream, level, block, device):
        copy_of(stream, 2, level, None, block, device).wait_send()

    def needs(some_chip, chunk):
        return (chunk <= some_chip) & (2 * chunk + 1 >= 2 * some_chip - window)

    def from_under(some_z, some_y, level):
        return (some_y == 0) & (some_z - level == depth) & needs(2 * some_z, 2 * level + 1)

    def spared(level):
        return (z == 2) & (y == 1) & (level == 0) if quick else False

    def climbs(level):
        return (z < levels - 1) & (z - level < depth) & jnp.logical_not(spared(level))

    def crosses(level):
        direct = needs(2 * z + 1 - y, 2 * level + y) & jnp.logical_not(from_under(z, 1 - y, level))
        return direct & jnp.logical_not(spared(level))

    def crossed(level):
        return needs(chip, 2 * level + 1 - y)

    def passes(level):
        return (z < levels - 1) & from_under(z + 1, y, level)

    def own(level):
        return level * 4 + r

    def other(level):
        return level * 4 + 2 * (1 - y) + c

    def relay(level, piece):
        @pl.when(climbs(level))
        def _():
            start(0, 0, level, piece, own(level), up)

        @pl.when(crosses(level))
        def _():
            start(1, 1, level, piece, own(level), across)

        start(2, 2, level, piece, own(level), partner)

    def from_below(level):
        def plain():
            for piece in range(len(pieces)):
                arrived(0, level, piece, own(level), up)
                relay(level, piece)

        if not quick:
            plain()
            return
        pl.when(jnp.logical_not(source))(plain)

        @pl.when(source)
        def _():
            for piece in range(len(pieces)):
                arrived(0, level, piece, own(level), up)
                start(4, 1, level, piece, own(level), me + 2)
                start(1, 1, level, piece, own(level), across)
                start(2, 2, level, piece, own(level), partner)
            for piece in range(len(pieces)):
                start(0, 0, level, piece, own(level), up)
            pl.semaphore_wait(ready_sem, 1)
            for piece in range(len(pieces)):
                start(5, 0, level, piece, own(level), me + 8)

    def from_across(level):
        @pl.when(crossed(level))
        def _():
            for piece in range(len(pieces)):
                arrived(1, level, piece, other(level), across)

                @pl.when(passes(level))
                def _():
                    start(4, 1, level, piece, other(level), up)

                start(3, 3, level, piece, other(level), partner)

    def own_pair(level):
        arrived(2, level, None, level * 4 + 2 * y + 1 - c, partner)

    def other_pair(level):
        @pl.when(crossed(level))
        def _():
            arrived(3, level, None, level * 4 + 2 * (1 - y) + 1 - c, partner)

    def finish(level):
        @pl.when(climbs(level))
        def _():
            sent(0, level, own(level), up)

        @pl.when(crosses(level))
        def _():
            sent(1, level, own(level), across)

        sent(2, level, own(level), partner)
        if quick:

            @pl.when(source & (level == 0))
            def _():
                sent(4, level, own(level), me + 2)
                sent(5, level, own(level), me + 8)

        @pl.when(crossed(level))
        def _():
            sent(3, level, other(level), partner)

            @pl.when(passes(level))
            def _():
                sent(4, level, other(level), up)

    doc_fill.wait()
    ids = docs[...]
    bounds = [jnp.sum(jnp.where(ids < doc, 1.0, 0.0), keepdims=True) for doc in range(1, DOCS)]
    bounds = [jnp.broadcast_to(bound, (1, dim)) for bound in bounds]
    bounds.append(jnp.zeros((DOC_ROWS - len(bounds), dim), jnp.float32))
    kv[span(me, rows, DOC_ROWS), :] = jnp.concatenate(bounds, axis=0).astype(jnp.bfloat16)
    greeters = 2 + jnp.minimum(z, 1) + jnp.minimum(levels - 1 - z, 1)
    if quick:
        greeters = greeters + jnp.where(source | beyond, 1, 0)
    pl.semaphore_wait(barrier, greeters)
    if quick:

        @pl.when(beyond)
        def _():
            pl.semaphore_signal(
                ready_sem, inc=1, device_id={"ctx": me - 8}, device_id_type=pl.DeviceIdType.MESH
            )

    fills[0].wait()
    for piece in range(len(pieces)):
        if pieces[piece][0] == rows + DOC_ROWS:
            fills[1].wait()
        relay(z, piece)

    lane = lax.broadcasted_iota(jnp.int32, (rows, dim), 1)
    row = lax.broadcasted_iota(jnp.int32, (rows, dim), 0).astype(jnp.float32)

    def doc_of(block):
        bounds = kv[span(block, rows, DOC_ROWS), :].astype(jnp.float32)
        number = jnp.zeros((rows, dim), jnp.int32)
        for doc in range(1, DOCS):
            number = number + jnp.where(row >= bounds[doc - 1 : doc, :], 1, 0)
        return number

    query_marks = jnp.where(lane == doc_of(me), 0.0, HIDDEN).astype(jnp.bfloat16)
    query_fill.wait()
    for head in range(heads):
        here = slice(head * rows, (head + 1) * rows)
        qs[here, :dim] = q_ref[:, head * dim : (head + 1) * dim]
        qs[here, dim:] = query_marks

    tile_rows = TILE_HEADS * rows
    tiles = heads // TILE_HEADS

    def attend(blocks, first=False):
        ks, vs = [], []
        for block in blocks:
            marks = jnp.where(lane == doc_of(block), 1.0, 0.0).astype(jnp.bfloat16)
            ks.append(jnp.concatenate([kv[span(block, 0, rows), :], marks], axis=1))
            vs.append(jnp.concatenate([kv[span(block, rows + DOC_ROWS, rows), :], jnp.ones((rows, dim), jnp.bfloat16)], axis=1))
        k_block = jnp.concatenate(ks, axis=0)
        v_block = jnp.concatenate(vs, axis=0)
        length = k_block.shape[0]

        def scores(tile):
            return lax.dot_general(
                qs[tile * tile_rows : (tile + 1) * tile_rows, :],
                k_block,
                (((1,), (1,)), ((), ())),
                preferred_element_type=jnp.float32,
            )

        following = scores(0)
        for tile in range(tiles):
            s = following
            if tile + 1 < tiles:
                following = scores(tile + 1)
            here = slice(tile * tile_rows, (tile + 1) * tile_rows)
            if first:
                key_id = lax.broadcasted_iota(jnp.int32, (rows, rows), 1)
                query_id = lax.broadcasted_iota(jnp.int32, (rows, rows), 0)
                hide = jnp.where(key_id <= query_id, 0.0, HIDDEN)
                s = s + jnp.concatenate([hide] * TILE_HEADS, axis=0)
            new = jnp.broadcast_to(jnp.max(s, axis=1, keepdims=True), (tile_rows, dim))
            if not first:
                old = m_ref[here]
                new = jnp.maximum(old, new)
            m_ref[here] = new
            w = jnp.exp2((s - jnp.tile(new, (1, length // dim))) * scale)
            part = jnp.dot(w.astype(jnp.bfloat16), v_block, preferred_element_type=jnp.float32)
            if first:
                acc_ref[here] = part
            else:
                acc_ref[here] = (
                    acc_ref[here] * jnp.tile(jnp.exp2((old - new) * scale), (1, 2)) + part
                )

    attend([me], True)
    own_pair(z)

    @pl.when(c == 1)
    def _():
        attend([me - 1])

    def early(level):
        return jnp.logical_not(top) & (climbs(level) | crosses(level))

    def ahead(i, carry):
        pl.when(early(z - i))(lambda: from_below(z - i))
        return carry

    lax.fori_loop(1, last + 1, ahead, 0)

    def pair_of(level):
        return level * 4 + 2 * y + 1 - c

    def other_pair_of(level):
        return level * 4 + 2 * (1 - y) + 1 - c

    for i in range(1, depth + 1):

        @pl.when(z >= i)
        def _():
            level = z - i
            final = (z == i) | (i == depth)
            late = final & (y == 1)
            single = late & tail
            pairs = late & jnp.logical_not(tail)
            before = jnp.logical_not(late)
            both = before & crossed(level + 1)
            hooked = top & (y == 1) if i > 1 else False
            waits = jnp.logical_not(early(level))

            pl.when(before & waits & jnp.logical_not(hooked))(lambda: from_below(level))
            from_across(level + 1)
            pl.when(final & jnp.logical_not(top))(lambda: from_across(level))
            pl.when(pairs)(lambda: other_pair(level + 1))

            @pl.when(both | pairs)
            def _():
                attend(
                    [
                        jnp.where(both, own(level), other(level + 1)),
                        jnp.where(both, other(level + 1), other_pair_of(level + 1)),
                    ]
                )

            pl.when(pairs & waits)(lambda: from_below(level))
            if i + 1 < depth:
                last_but = z == i + 1
                pl.when(top & (y == 1) & jnp.logical_not(final | last_but))(
                    lambda: from_below(level - 1)
                )

            @pl.when(jnp.logical_not(single))
            def _():
                own_pair(level)
                pl.when(both)(lambda: other_pair(level + 1))
                attend(
                    [
                        jnp.where(both, pair_of(level), own(level)),
                        jnp.where(both, other_pair_of(level + 1), pair_of(level)),
                    ]
                )

    pl.when(z == 0)(lambda: from_across(z))

    @pl.when(jnp.logical_not(tail))
    def _():
        @pl.when(crossed(z - last))
        def _():
            other_pair(z - last)
            attend([other(z - last), other_pair_of(z - last)])

    def closing(turn, carry):
        level = z - last

        @pl.when(turn == 1)
        def _():
            from_below(level)
            other_pair(level + 1)

        pl.when(turn == 3)(lambda: own_pair(level))
        pl.when(turn == 4)(lambda: from_across(level))
        pl.when(turn == 5)(lambda: other_pair(level))
        theirs = (turn < 2) | (turn > 3)
        base = (level + jnp.where(turn < 2, 1, 0)) * 4 + 2 * jnp.where(theirs, 1 - y, y)
        block = base + jnp.where(turn % 2 == 0, c, 1 - c)

        @pl.when((block <= me) & (block >= me - window))
        def _():
            attend([block])

        return carry

    @pl.when(tail)
    def _():
        lax.fori_loop(4 - 4 * y, 6 - 2 * y, closing, 0)

    for head in range(heads):
        here = slice(head * rows, (head + 1) * rows)
        o_ref[:, head * dim : (head + 1) * dim] = (acc_ref[here, :dim] / acc_ref[here, dim:]).astype(
            o_ref.dtype
        )

    def drain(i, carry):
        finish(z - i)
        return carry

    lax.fori_loop(0, last + 1, drain, 0)


def solution(mesh):
    n = mesh.shape["ctx"]

    def on_device(queries, keys, values, doc_ids):
        rows, width = queries.shape
        dim = keys.shape[1]
        heads = width // dim
        levels = n // 4
        anywhere = pl.BlockSpec(memory_space=pl.ANY)
        return pl.pallas_call(
            functools.partial(kernel, n),
            out_shape=jax.ShapeDtypeStruct((rows, width), jnp.bfloat16),
            in_specs=[anywhere] * 4,
            out_specs=pl.BlockSpec(memory_space=pltpu.VMEM),
            scratch_shapes=[
                pltpu.VMEM((rows, width), jnp.bfloat16),
                pltpu.VMEM((n * (2 * rows + DOC_ROWS), dim), jnp.bfloat16),
                pltpu.VMEM((rows // dim, dim), jnp.int32),
                pltpu.VMEM((heads * rows, dim), jnp.float32),
                pltpu.VMEM((heads * rows, 2 * dim), jnp.float32),
                pltpu.VMEM((heads * rows, 2 * dim), jnp.bfloat16),
                pltpu.SemaphoreType.DMA((4,)),
                pltpu.SemaphoreType.DMA((4, levels)),
                pltpu.SemaphoreType.DMA((2, levels, PIECES)),
                pltpu.SemaphoreType.DMA((2, levels)),
                pltpu.SemaphoreType.DMA((2,)),
                pltpu.SemaphoreType.REGULAR,
            ],
            compiler_params=pltpu.CompilerParams(collective_id=0, has_side_effects=True, vmem_limit_bytes=16 * 1024 * 1024),
        )(*[pltpu.with_memory_space_constraint(a, pltpu.HBM) for a in (queries, keys, values, doc_ids.reshape(rows // dim, dim))])

    spec = P(("groups", "ctx"), None)
    return jax.shard_map(
        on_device,
        mesh=mesh,
        in_specs=(spec, spec, spec, P(("groups", "ctx"))),
        out_specs=spec,
        check_vma=False,
    )
```

```python
import functools

import jax
import jax.numpy as jnp
from jax import lax
from jax.experimental import pallas as pl
from jax.experimental.pallas import tpu as pltpu
from jax.sharding import PartitionSpec as P

HIDDEN = -1e30
LOG2E = 1.4426950408889634
DOCS = 3
DOC_ROWS = 16
PIECES = 4
TILE_HEADS = 2


def kernel(
    n,
    q_hbm,
    k_hbm,
    v_hbm,
    d_hbm,
    o_ref,
    q_ref,
    kv,
    docs,
    m_ref,
    acc_ref,
    qs,
    fill_sem,
    send_kv,
    recv_kv,
    recv_pair,
    send_far,
    ready_sem,
):
    rows, width = q_hbm.shape
    dim = k_hbm.shape[1]
    heads = width // dim
    levels = n // 4
    window = 3 * n // 4
    depth = (window + 3) // 4
    me = lax.axis_index("ctx")
    z = me // 4
    r = me % 4
    y = r // 2
    c = r % 2
    chip = me // 2
    up = me + 4
    across = z * 4 + (1 - y) * 2 + c
    partner = z * 4 + y * 2 + (1 - c)
    scale = dim ** (-0.5) * LOG2E
    top = z == levels - 1
    tail = top & (z >= depth)
    last = jnp.minimum(z, depth)
    quick = levels == 4
    source = (z == 1) & (y == 1) if quick else False
    aside = (z == 2) & (y == 0) if quick else False
    beyond = (z == 3) & (y == 1) if quick else False

    barrier = pltpu.get_barrier_semaphore()

    def greet(device):
        pl.semaphore_signal(
            barrier, inc=1, device_id={"ctx": device}, device_id_type=pl.DeviceIdType.MESH
        )

    @pl.when(z > 0)
    def _():
        greet(me - 4)

    @pl.when(z < levels - 1)
    def _():
        greet(up)

    greet(across)
    greet(partner)
    if quick:

        @pl.when(aside)
        def _():
            greet(me - 2)

        @pl.when(source)
        def _():
            greet(me + 8)

    assert rows <= 256 and rows % dim == 0
    stride = 2 * rows + DOC_ROWS
    half = rows // 2
    pieces = [(0, half), (half, half + DOC_ROWS), (rows + DOC_ROWS, half), (rows + DOC_ROWS + half, half)]

    def span(block, first=0, count=stride):
        return pl.ds(pl.multiple_of(block * stride + first, DOC_ROWS), count)

    doc_fill = pltpu.make_async_copy(d_hbm, docs, fill_sem.at[2])
    doc_fill.start()
    fills = [
        pltpu.make_async_copy(k_hbm, kv.at[span(me, 0, rows), :], fill_sem.at[0]),
        pltpu.make_async_copy(v_hbm, kv.at[span(me, rows + DOC_ROWS, rows), :], fill_sem.at[1]),
    ]
    for fill in fills:
        fill.start()
    query_fill = pltpu.make_async_copy(q_hbm, q_ref, fill_sem.at[3])
    query_fill.start()

    def landing(lands, level, piece):
        return recv_kv.at[lands, level, piece] if lands < 2 else recv_pair.at[lands - 2, level]

    def copy_of(stream, lands, level, piece, block, device):
        place = span(block) if piece is None else span(block, *pieces[piece])
        return pltpu.make_async_remote_copy(
            src_ref=kv.at[place, :],
            dst_ref=kv.at[place, :],
            send_sem=send_kv.at[stream, level] if stream < 4 else send_far.at[stream - 4],
            recv_sem=landing(lands, level, piece),
            device_id={"ctx": device},
            device_id_type=pl.DeviceIdType.MESH,
        )

    def start(stream, lands, level, piece, block, device):
        copy_of(stream, lands, level, piece, block, device).start()

    def arrived(lands, level, piece, block, device):
        copy_of(lands, lands, level, piece, block, device).wait_recv()

    def sent(stream, level, block, device):
        copy_of(stream, 2, level, None, block, device).wait_send()

    def needs(some_chip, chunk):
        return (chunk <= some_chip) & (2 * chunk + 1 >= 2 * some_chip - window)

    def from_under(some_z, some_y, level):
        return (some_y == 0) & (some_z - level == depth) & needs(2 * some_z, 2 * level + 1)

    def spared(level):
        return (z == 2) & (y == 1) & (level == 0) if quick else False

    def climbs(level):
        return (z < levels - 1) & (z - level < depth) & jnp.logical_not(spared(level))

    def crosses(level):
        direct = needs(2 * z + 1 - y, 2 * level + y) & jnp.logical_not(from_under(z, 1 - y, level))
        return direct & jnp.logical_not(spared(level))

    def crossed(level):
        return needs(chip, 2 * level + 1 - y)

    def passes(level):
        return (z < levels - 1) & from_under(z + 1, y, level)

    def own(level):
        return level * 4 + r

    def other(level):
        return level * 4 + 2 * (1 - y) + c

    def relay(level, piece):
        @pl.when(climbs(level))
        def _():
            start(0, 0, level, piece, own(level), up)

        @pl.when(crosses(level))
        def _():
            start(1, 1, level, piece, own(level), across)

        if piece == len(pieces) - 1:
            start(2, 2, level, None, own(level), partner)

    def from_below(level):
        def plain():
            for piece in range(len(pieces)):
                arrived(0, level, piece, own(level), up)
                relay(level, piece)

        if not quick:
            plain()
            return
        pl.when(jnp.logical_not(source))(plain)

        @pl.when(source)
        def _():
            for piece in range(len(pieces)):
                arrived(0, level, piece, own(level), up)
                start(4, 1, level, piece, own(level), me + 2)
                start(1, 1, level, piece, own(level), across)
            start(2, 2, level, None, own(level), partner)
            for piece in range(len(pieces)):
                start(0, 0, level, piece, own(level), up)
            pl.semaphore_wait(ready_sem, 1)
            for piece in range(len(pieces)):
                start(5, 0, level, piece, own(level), me + 8)

    def from_across(level):
        @pl.when(crossed(level))
        def _():
            for piece in range(len(pieces)):
                arrived(1, level, piece, other(level), across)

                @pl.when(passes(level))
                def _():
                    start(4, 1, level, piece, other(level), up)

            start(3, 3, level, None, other(level), partner)

    def own_pair(level):
        arrived(2, level, None, level * 4 + 2 * y + 1 - c, partner)

    def other_pair(level):
        @pl.when(crossed(level))
        def _():
            arrived(3, level, None, level * 4 + 2 * (1 - y) + 1 - c, partner)

    def finish(level):
        @pl.when(climbs(level))
        def _():
            sent(0, level, own(level), up)

        @pl.when(crosses(level))
        def _():
            sent(1, level, own(level), across)

        sent(2, level, own(level), partner)
        if quick:

            @pl.when(source & (level == 0))
            def _():
                sent(4, level, own(level), me + 2)
                sent(5, level, own(level), me + 8)

        @pl.when(crossed(level))
        def _():
            sent(3, level, other(level), partner)

            @pl.when(passes(level))
            def _():
                sent(4, level, other(level), up)

    doc_fill.wait()
    ids = docs[...]
    bounds = [jnp.sum(jnp.where(ids < doc, 1.0, 0.0), keepdims=True) for doc in range(1, DOCS)]
    bounds = [jnp.broadcast_to(bound, (1, dim)) for bound in bounds]
    bounds.append(jnp.zeros((DOC_ROWS - len(bounds), dim), jnp.float32))
    kv[span(me, rows, DOC_ROWS), :] = jnp.concatenate(bounds, axis=0).astype(jnp.bfloat16)
    greeters = 2 + jnp.minimum(z, 1) + jnp.minimum(levels - 1 - z, 1)
    if quick:
        greeters = greeters + jnp.where(source | beyond, 1, 0)
    pl.semaphore_wait(barrier, greeters)
    if quick:

        @pl.when(beyond)
        def _():
            pl.semaphore_signal(
                ready_sem, inc=1, device_id={"ctx": me - 8}, device_id_type=pl.DeviceIdType.MESH
            )

    fills[0].wait()
    for piece in range(len(pieces)):
        if pieces[piece][0] == rows + DOC_ROWS:
            fills[1].wait()
        relay(z, piece)

    lane = lax.broadcasted_iota(jnp.int32, (rows, dim), 1)
    row = lax.broadcasted_iota(jnp.int32, (rows, dim), 0).astype(jnp.float32)

    def doc_of(block):
        bounds = kv[span(block, rows, DOC_ROWS), :].astype(jnp.float32)
        number = jnp.zeros((rows, dim), jnp.int32)
        for doc in range(1, DOCS):
            number = number + jnp.where(row >= bounds[doc - 1 : doc, :], 1, 0)
        return number

    query_marks = jnp.where(lane == doc_of(me), 0.0, HIDDEN).astype(jnp.bfloat16)
    query_fill.wait()
    for head in range(heads):
        here = slice(head * rows, (head + 1) * rows)
        qs[here, :dim] = q_ref[:, head * dim : (head + 1) * dim]
        qs[here, dim:] = query_marks

    tile_rows = TILE_HEADS * rows
    tiles = heads // TILE_HEADS

    def attend(blocks, first=False):
        ks, vs = [], []
        for block in blocks:
            marks = jnp.where(lane == doc_of(block), 1.0, 0.0).astype(jnp.bfloat16)
            ks.append(jnp.concatenate([kv[span(block, 0, rows), :], marks], axis=1))
            vs.append(jnp.concatenate([kv[span(block, rows + DOC_ROWS, rows), :], jnp.ones((rows, dim), jnp.bfloat16)], axis=1))
        k_block = jnp.concatenate(ks, axis=0)
        v_block = jnp.concatenate(vs, axis=0)
        length = k_block.shape[0]

        def scores(tile):
            return lax.dot_general(
                qs[tile * tile_rows : (tile + 1) * tile_rows, :],
                k_block,
                (((1,), (1,)), ((), ())),
                preferred_element_type=jnp.float32,
            )

        following = scores(0)
        for tile in range(tiles):
            s = following
            if tile + 1 < tiles:
                following = scores(tile + 1)
            here = slice(tile * tile_rows, (tile + 1) * tile_rows)
            if first:
                key_id = lax.broadcasted_iota(jnp.int32, (rows, rows), 1)
                query_id = lax.broadcasted_iota(jnp.int32, (rows, rows), 0)
                hide = jnp.where(key_id <= query_id, 0.0, HIDDEN)
                s = s + jnp.concatenate([hide] * TILE_HEADS, axis=0)
            new = jnp.broadcast_to(jnp.max(s, axis=1, keepdims=True), (tile_rows, dim))
            if not first:
                old = m_ref[here]
                new = jnp.maximum(old, new)
            m_ref[here] = new
            w = jnp.exp2((s - jnp.tile(new, (1, length // dim))) * scale)
            part = jnp.dot(w.astype(jnp.bfloat16), v_block, preferred_element_type=jnp.float32)
            if first:
                acc_ref[here] = part
            else:
                acc_ref[here] = (
                    acc_ref[here] * jnp.tile(jnp.exp2((old - new) * scale), (1, 2)) + part
                )

    attend([me], True)
    own_pair(z)

    @pl.when(c == 1)
    def _():
        attend([me - 1])

    def early(level):
        return jnp.logical_not(top) & (climbs(level) | crosses(level))

    def ahead(i, carry):
        pl.when(early(z - i))(lambda: from_below(z - i))
        return carry

    lax.fori_loop(1, last + 1, ahead, 0)

    def pair_of(level):
        return level * 4 + 2 * y + 1 - c

    def other_pair_of(level):
        return level * 4 + 2 * (1 - y) + 1 - c

    for i in range(1, depth + 1):

        @pl.when(z >= i)
        def _():
            level = z - i
            final = (z == i) | (i == depth)
            late = final & (y == 1)
            pairs = late & jnp.logical_not(tail)
            before = jnp.logical_not(pairs)
            both = before & crossed(level + 1)
            hooked = top & (y == 1) if i > 1 else False
            waits = jnp.logical_not(early(level))

            closing = late & tail
            pl.when(before & waits & jnp.logical_not(hooked | closing))(lambda: from_below(level))
            far = final & jnp.logical_not(top) & (y == 0)
            pl.when(far)(lambda: from_across(level))
            from_across(level + 1)
            pl.when(closing)(lambda: from_below(level))
            pl.when(pairs)(lambda: from_across(level))
            pl.when(pairs)(lambda: other_pair(level + 1))

            @pl.when(both | pairs)
            def _():
                attend(
                    [
                        jnp.where(both, own(level), other(level + 1)),
                        jnp.where(both, other(level + 1), other_pair_of(level + 1)),
                    ]
                )

            if i + 1 < depth:
                last_but = z == i + 1
                pl.when(top & (y == 1) & jnp.logical_not(final | last_but))(
                    lambda: from_below(level - 1)
                )

            pl.when(final & tail)(lambda: from_across(level))
            pl.when(pairs & waits)(lambda: from_below(level))

            @pl.when(before | crossed(level))
            def _():
                pl.when(before)(lambda: own_pair(level))
                pl.when(both)(lambda: other_pair(level + 1))
                pl.when(pairs)(lambda: other_pair(level))
                attend(
                    [
                        jnp.where(both, pair_of(level), jnp.where(pairs, other(level), own(level))),
                        jnp.where(
                            both,
                            other_pair_of(level + 1),
                            jnp.where(pairs, other_pair_of(level), pair_of(level)),
                        ),
                    ]
                )

    level = z - last
    pairs = (y == 1) & (z > 0) & jnp.logical_not(tail)
    pl.when((z == 0) | (top & jnp.logical_not(tail) & (y == 0)))(lambda: from_across(level))

    pl.when(pairs)(lambda: own_pair(level))
    pl.when(jnp.logical_not(pairs))(lambda: other_pair(level))

    @pl.when(pairs | crossed(level))
    def _():
        attend(
            [
                jnp.where(pairs, own(level), other(level)),
                jnp.where(pairs, pair_of(level), other_pair_of(level)),
            ]
        )

    for head in range(heads):
        here = slice(head * rows, (head + 1) * rows)
        o_ref[:, head * dim : (head + 1) * dim] = (acc_ref[here, :dim] / acc_ref[here, dim:]).astype(
            o_ref.dtype
        )

    def drain(i, carry):
        finish(z - i)
        return carry

    lax.fori_loop(0, last + 1, drain, 0)


def solution(mesh):
    n = mesh.shape["ctx"]

    def on_device(queries, keys, values, doc_ids):
        rows, width = queries.shape
        dim = keys.shape[1]
        heads = width // dim
        levels = n // 4
        anywhere = pl.BlockSpec(memory_space=pl.ANY)
        return pl.pallas_call(
            functools.partial(kernel, n),
            out_shape=jax.ShapeDtypeStruct((rows, width), jnp.bfloat16),
            in_specs=[anywhere] * 4,
            out_specs=pl.BlockSpec(memory_space=pltpu.VMEM),
            scratch_shapes=[
                pltpu.VMEM((rows, width), jnp.bfloat16),
                pltpu.VMEM((n * (2 * rows + DOC_ROWS), dim), jnp.bfloat16),
                pltpu.VMEM((rows // dim, dim), jnp.int32),
                pltpu.VMEM((heads * rows, dim), jnp.float32),
                pltpu.VMEM((heads * rows, 2 * dim), jnp.float32),
                pltpu.VMEM((heads * rows, 2 * dim), jnp.bfloat16),
                pltpu.SemaphoreType.DMA((4,)),
                pltpu.SemaphoreType.DMA((4, levels)),
                pltpu.SemaphoreType.DMA((2, levels, PIECES)),
                pltpu.SemaphoreType.DMA((2, levels)),
                pltpu.SemaphoreType.DMA((2,)),
                pltpu.SemaphoreType.REGULAR,
            ],
            compiler_params=pltpu.CompilerParams(collective_id=0, has_side_effects=True, vmem_limit_bytes=16 * 1024 * 1024),
        )(*[pltpu.with_memory_space_constraint(a, pltpu.HBM) for a in (queries, keys, values, doc_ids.reshape(rows // dim, dim))])

    spec = P(("groups", "ctx"), None)
    return jax.shard_map(
        on_device,
        mesh=mesh,
        in_specs=(spec, spec, spec, P(("groups", "ctx"))),
        out_specs=spec,
        check_vma=False,
    )
```

```python
import functools

import jax
import jax.numpy as jnp
from jax import lax
from jax.experimental import pallas as pl
from jax.experimental.pallas import tpu as pltpu
from jax.sharding import PartitionSpec as P

HIDDEN = -1e30
LOG2E = 1.4426950408889634
DOCS = 3
DOC_ROWS = 16
PIECES = 4
FAR = -1
TILE_HEADS = 2


def kernel(
    n,
    q_hbm,
    k_hbm,
    v_hbm,
    d_hbm,
    o_ref,
    q_ref,
    kv,
    docs,
    m_ref,
    acc_ref,
    qs,
    fill_sem,
    send_kv,
    recv_kv,
    recv_other,
    recv_far,
    recv_pair,
    send_far,
    ready_sem,
):
    rows, width = q_hbm.shape
    dim = k_hbm.shape[1]
    heads = width // dim
    levels = n // 4
    window = 3 * n // 4
    depth = (window + 3) // 4
    me = lax.axis_index("ctx")
    z = me // 4
    r = me % 4
    y = r // 2
    c = r % 2
    chip = me // 2
    up = me + 4
    across = z * 4 + (1 - y) * 2 + c
    partner = z * 4 + y * 2 + (1 - c)
    scale = dim ** (-0.5) * LOG2E
    top = z == levels - 1
    tail = top & (z >= depth)
    last = jnp.minimum(z, depth)
    quick = levels == 4
    source = (z == 1) & (y == 1) if quick else False
    aside = (z == 2) & (y == 0) if quick else False
    beyond = (z == 3) & (y == 1) if quick else False

    barrier = pltpu.get_barrier_semaphore()

    def greet(device):
        pl.semaphore_signal(
            barrier, inc=1, device_id={"ctx": device}, device_id_type=pl.DeviceIdType.MESH
        )

    @pl.when(z > 0)
    def _():
        greet(me - 4)

    @pl.when(z < levels - 1)
    def _():
        greet(up)

    greet(across)
    greet(partner)
    if quick:

        @pl.when(aside)
        def _():
            greet(me - 2)

        @pl.when(source)
        def _():
            greet(me + 8)

    assert rows <= 256 and rows % dim == 0
    stride = 2 * rows + DOC_ROWS
    half = rows // 2
    pieces = [(0, half), (half, half + DOC_ROWS), (rows + DOC_ROWS, half), (rows + DOC_ROWS + half, half)]

    def span(block, first=0, count=stride):
        return pl.ds(pl.multiple_of(block * stride + first, DOC_ROWS), count)

    doc_fill = pltpu.make_async_copy(d_hbm, docs, fill_sem.at[2])
    doc_fill.start()
    fills = [
        pltpu.make_async_copy(k_hbm, kv.at[span(me, 0, rows), :], fill_sem.at[0]),
        pltpu.make_async_copy(v_hbm, kv.at[span(me, rows + DOC_ROWS, rows), :], fill_sem.at[1]),
    ]
    for fill in fills:
        fill.start()
    query_fill = pltpu.make_async_copy(q_hbm, q_ref, fill_sem.at[3])
    query_fill.start()

    def landing(lands, level, piece, to_top):
        if lands > 1:
            return recv_pair.at[lands - 2, level]
        if lands == FAR:
            return recv_far.at[piece]
        if lands == 0:
            whole = (level == 0) & to_top if quick else False
            return recv_kv.at[level, jnp.where(whole, 0, piece or 0)]
        return recv_other.at[level, 0 if quick else piece]

    def copy_of(stream, lands, level, piece, block, device, to_top=False):
        place = span(block) if piece is None else span(block, *pieces[piece])
        return pltpu.make_async_remote_copy(
            src_ref=kv.at[place, :],
            dst_ref=kv.at[place, :],
            send_sem=send_kv.at[stream // 3, level] if stream < 4 else send_far.at[stream - 4],
            recv_sem=landing(lands, level, piece, to_top),
            device_id={"ctx": device},
            device_id_type=pl.DeviceIdType.MESH,
        )

    def start(stream, lands, level, piece, block, device):
        to_top = stream == 5 or (z == levels - 2 if stream == 0 else False)
        copy_of(stream, lands, level, piece, block, device, to_top).start()

    def arrived(lands, level, piece, block, device):
        copy_of(max(lands, 0), lands, level, piece, block, device, top).wait_recv()

    def sent(stream, level, block, device):
        copy_of(stream, 2, level, None, block, device).wait_send()

    def needs(some_chip, chunk):
        return (chunk <= some_chip) & (2 * chunk + 1 >= 2 * some_chip - window)

    def from_under(some_z, some_y, level):
        return (some_y == 0) & (some_z - level == depth) & needs(2 * some_z, 2 * level + 1)

    def spared(level):
        return (z == 2) & (y == 1) & (level == 0) if quick else False

    def climbs(level):
        return (z < levels - 1) & (z - level < depth) & jnp.logical_not(spared(level))

    def crosses(level):
        direct = needs(2 * z + 1 - y, 2 * level + y) & jnp.logical_not(from_under(z, 1 - y, level))
        return direct & jnp.logical_not(spared(level))

    def crossed(level):
        return needs(chip, 2 * level + 1 - y)

    def passes(level):
        return (z < levels - 1) & from_under(z + 1, y, level)

    def own(level):
        return level * 4 + r

    def other(level):
        return level * 4 + 2 * (1 - y) + c

    def relay(level, piece):
        @pl.when(climbs(level))
        def _():
            start(0, 0, level, piece, own(level), up)

        @pl.when(crosses(level))
        def _():
            start(1, 1, level, piece, own(level), across)

        if piece == len(pieces) - 1:
            start(2, 2, level, None, own(level), partner)

    def from_below(level):
        def plain():
            for piece in range(len(pieces)):
                arrived(0, level, piece, own(level), up)
                relay(level, piece)

        def whole():
            arrived(0, level, None, own(level), up)
            start(2, 2, level, None, own(level), partner)

        if not quick:
            plain()
            return
        ends = top & (level == 0)
        pl.when(ends)(whole)
        pl.when(jnp.logical_not(source | ends))(plain)

        @pl.when(source)
        def _():
            for piece in range(len(pieces)):
                arrived(0, level, piece, own(level), up)
                start(4, FAR, level, piece, own(level), me + 2)
                start(1, 1, level, piece, own(level), across)
            start(2, 2, level, None, own(level), partner)
            for piece in range(len(pieces)):
                start(0, 0, level, piece, own(level), up)
            pl.semaphore_wait(ready_sem, 1)
            for piece in range(len(pieces)):
                start(5, 0, level, piece, own(level), me + 8)

    def from_across(level):
        def piecewise(lands):
            for piece in range(len(pieces)):
                arrived(lands, level, piece, other(level), across)

                @pl.when(passes(level))
                def _():
                    start(4, 1, level, piece, other(level), up)

        @pl.when(crossed(level))
        def _():
            if quick:
                pl.when(passes(level))(lambda: piecewise(FAR))
                pl.when(jnp.logical_not(passes(level)))(
                    lambda: arrived(1, level, None, other(level), across)
                )
            else:
                piecewise(1)
            start(3, 3, level, None, other(level), partner)

    def own_pair(level):
        arrived(2, level, None, level * 4 + 2 * y + 1 - c, partner)

    def other_pair(level):
        @pl.when(crossed(level))
        def _():
            arrived(3, level, None, level * 4 + 2 * (1 - y) + 1 - c, partner)

    def finish(level):
        copies = 1 + jnp.where(climbs(level), 1, 0) + jnp.where(crosses(level), 1, 0)
        for many in range(1, 4):

            @pl.when(copies == many)
            def _():
                everything = kv.at[pl.ds(0, many * stride), :]
                pltpu.make_async_remote_copy(
                    src_ref=everything,
                    dst_ref=everything,
                    send_sem=send_kv.at[0, level],
                    recv_sem=recv_pair.at[0, level],
                    device_id={"ctx": partner},
                    device_id_type=pl.DeviceIdType.MESH,
                ).wait_send()

        if quick:

            @pl.when(source & (level == 0))
            def _():
                sent(4, level, own(level), me + 2)
                sent(5, level, own(level), me + 8)

        @pl.when(crossed(level))
        def _():
            sent(3, level, other(level), partner)

            @pl.when(passes(level))
            def _():
                sent(4, level, other(level), up)

    doc_fill.wait()
    ids = docs[...]
    bounds = [jnp.sum(jnp.where(ids < doc, 1.0, 0.0), keepdims=True) for doc in range(1, DOCS)]
    bounds = [jnp.broadcast_to(bound, (1, dim)) for bound in bounds]
    bounds.append(jnp.zeros((DOC_ROWS - len(bounds), dim), jnp.float32))
    kv[span(me, rows, DOC_ROWS), :] = jnp.concatenate(bounds, axis=0).astype(jnp.bfloat16)
    greeters = 2 + jnp.minimum(z, 1) + jnp.minimum(levels - 1 - z, 1)
    if quick:
        greeters = greeters + jnp.where(source | beyond, 1, 0)
    pl.semaphore_wait(barrier, greeters)
    if quick:

        @pl.when(beyond)
        def _():
            pl.semaphore_signal(
                ready_sem, inc=1, device_id={"ctx": me - 8}, device_id_type=pl.DeviceIdType.MESH
            )

    fills[0].wait()
    for piece in range(len(pieces)):
        if pieces[piece][0] == rows + DOC_ROWS:
            fills[1].wait()
        relay(z, piece)

    lane = lax.broadcasted_iota(jnp.int32, (rows, dim), 1)
    row = lax.broadcasted_iota(jnp.int32, (rows, dim), 0).astype(jnp.float32)

    def doc_of(block):
        bounds = kv[span(block, rows, DOC_ROWS), :].astype(jnp.float32)
        number = jnp.zeros((rows, dim), jnp.int32)
        for doc in range(1, DOCS):
            number = number + jnp.where(row >= bounds[doc - 1 : doc, :], 1, 0)
        return number

    query_marks = jnp.where(lane == doc_of(me), 0.0, HIDDEN).astype(jnp.bfloat16)
    query_fill.wait()
    for head in range(heads):
        here = slice(head * rows, (head + 1) * rows)
        qs[here, :dim] = q_ref[:, head * dim : (head + 1) * dim]
        qs[here, dim:] = query_marks

    tile_rows = TILE_HEADS * rows
    tiles = heads // TILE_HEADS

    def attend(blocks, first=False):
        ks, vs = [], []
        for block in blocks:
            marks = jnp.where(lane == doc_of(block), 1.0, 0.0).astype(jnp.bfloat16)
            ks.append(jnp.concatenate([kv[span(block, 0, rows), :], marks], axis=1))
            vs.append(jnp.concatenate([kv[span(block, rows + DOC_ROWS, rows), :], jnp.ones((rows, dim), jnp.bfloat16)], axis=1))
        k_block = jnp.concatenate(ks, axis=0)
        v_block = jnp.concatenate(vs, axis=0)
        length = k_block.shape[0]

        def scores(tile):
            return lax.dot_general(
                qs[tile * tile_rows : (tile + 1) * tile_rows, :],
                k_block,
                (((1,), (1,)), ((), ())),
                preferred_element_type=jnp.float32,
            )

        following = scores(0)
        for tile in range(tiles):
            s = following
            if tile + 1 < tiles:
                following = scores(tile + 1)
            here = slice(tile * tile_rows, (tile + 1) * tile_rows)
            if first:
                key_id = lax.broadcasted_iota(jnp.int32, (rows, rows), 1)
                query_id = lax.broadcasted_iota(jnp.int32, (rows, rows), 0)
                hide = jnp.where(key_id <= query_id, 0.0, HIDDEN)
                s = s + jnp.concatenate([hide] * TILE_HEADS, axis=0)
            new = jnp.broadcast_to(jnp.max(s, axis=1, keepdims=True), (tile_rows, dim))
            if not first:
                old = m_ref[here]
                new = jnp.maximum(old, new)
            m_ref[here] = new
            w = jnp.exp2((s - jnp.tile(new, (1, length // dim))) * scale)
            part = jnp.dot(w.astype(jnp.bfloat16), v_block, preferred_element_type=jnp.float32)
            if first:
                acc_ref[here] = part
            else:
                acc_ref[here] = (
                    acc_ref[here] * jnp.tile(jnp.exp2((old - new) * scale), (1, 2)) + part
                )

    attend([me], True)
    own_pair(z)

    @pl.when(c == 1)
    def _():
        attend([me - 1])

    def early(level):
        return jnp.logical_not(top) & (climbs(level) | crosses(level))

    def ahead(i, carry):
        pl.when(early(z - i))(lambda: from_below(z - i))
        return carry

    lax.fori_loop(1, last + 1, ahead, 0)

    def pair_of(level):
        return level * 4 + 2 * y + 1 - c

    def other_pair_of(level):
        return level * 4 + 2 * (1 - y) + 1 - c

    for i in range(1, depth + 1):

        @pl.when(z >= i)
        def _():
            level = z - i
            final = (z == i) | (i == depth)
            late = final & (y == 1)
            pairs = late & jnp.logical_not(tail)
            before = jnp.logical_not(pairs)
            both = before & crossed(level + 1)
            hooked = top & (y == 1) if i > 1 else False
            waits = jnp.logical_not(early(level))

            closing = late & tail
            pl.when(before & waits & jnp.logical_not(hooked | closing))(lambda: from_below(level))
            far = final & jnp.logical_not(top) & (y == 0)
            pl.when(far)(lambda: from_across(level))
            from_across(level + 1)
            pl.when(closing)(lambda: from_below(level))
            pl.when(pairs)(lambda: from_across(level))
            pl.when(pairs)(lambda: other_pair(level + 1))

            @pl.when(both | pairs)
            def _():
                attend(
                    [
                        jnp.where(both, own(level), other(level + 1)),
                        jnp.where(both, other(level + 1), other_pair_of(level + 1)),
                    ]
                )

            if i + 1 < depth:
                last_but = z == i + 1
                pl.when(top & (y == 1) & jnp.logical_not(final | last_but))(
                    lambda: from_below(level - 1)
                )

            pl.when(final & tail)(lambda: from_across(level))
            pl.when(pairs & waits)(lambda: from_below(level))

            @pl.when(before | crossed(level))
            def _():
                pl.when(before)(lambda: own_pair(level))
                pl.when(both)(lambda: other_pair(level + 1))
                pl.when(pairs)(lambda: other_pair(level))
                attend(
                    [
                        jnp.where(both, pair_of(level), jnp.where(pairs, other(level), own(level))),
                        jnp.where(
                            both,
                            other_pair_of(level + 1),
                            jnp.where(pairs, other_pair_of(level), pair_of(level)),
                        ),
                    ]
                )

    level = z - last
    pairs = (y == 1) & (z > 0) & jnp.logical_not(tail)
    pl.when((z == 0) | (top & jnp.logical_not(tail) & (y == 0)))(lambda: from_across(level))

    pl.when(pairs)(lambda: own_pair(level))
    pl.when(jnp.logical_not(pairs))(lambda: other_pair(level))

    @pl.when(pairs | crossed(level))
    def _():
        attend(
            [
                jnp.where(pairs, own(level), other(level)),
                jnp.where(pairs, pair_of(level), other_pair_of(level)),
            ]
        )

    for head in range(heads):
        here = slice(head * rows, (head + 1) * rows)
        o_ref[:, head * dim : (head + 1) * dim] = (acc_ref[here, :dim] / acc_ref[here, dim:]).astype(
            o_ref.dtype
        )

    def drain(i, carry):
        finish(z - i)
        return carry

    lax.fori_loop(0, last + 1, drain, 0)


def solution(mesh):
    n = mesh.shape["ctx"]

    def on_device(queries, keys, values, doc_ids):
        rows, width = queries.shape
        dim = keys.shape[1]
        heads = width // dim
        levels = n // 4
        anywhere = pl.BlockSpec(memory_space=pl.ANY)
        return pl.pallas_call(
            functools.partial(kernel, n),
            out_shape=jax.ShapeDtypeStruct((rows, width), jnp.bfloat16),
            in_specs=[anywhere] * 4,
            out_specs=pl.BlockSpec(memory_space=pltpu.VMEM),
            scratch_shapes=[
                pltpu.VMEM((rows, width), jnp.bfloat16),
                pltpu.VMEM((n * (2 * rows + DOC_ROWS), dim), jnp.bfloat16),
                pltpu.VMEM((rows // dim, dim), jnp.int32),
                pltpu.VMEM((heads * rows, dim), jnp.float32),
                pltpu.VMEM((heads * rows, 2 * dim), jnp.float32),
                pltpu.VMEM((heads * rows, 2 * dim), jnp.bfloat16),
                pltpu.SemaphoreType.DMA((4,)),
                pltpu.SemaphoreType.DMA((2, levels)),
                pltpu.SemaphoreType.DMA((levels, PIECES)),
                pltpu.SemaphoreType.DMA((levels, 1 if levels == 4 else PIECES)),
                pltpu.SemaphoreType.DMA((PIECES,)),
                pltpu.SemaphoreType.DMA((2, levels)),
                pltpu.SemaphoreType.DMA((2,)),
                pltpu.SemaphoreType.REGULAR,
            ],
            compiler_params=pltpu.CompilerParams(collective_id=0, has_side_effects=True, vmem_limit_bytes=16 * 1024 * 1024),
        )(*[pltpu.with_memory_space_constraint(a, pltpu.HBM) for a in (queries, keys, values, doc_ids.reshape(rows // dim, dim))])

    spec = P(("groups", "ctx"), None)
    return jax.shard_map(
        on_device,
        mesh=mesh,
        in_specs=(spec, spec, spec, P(("groups", "ctx"))),
        out_specs=spec,
        check_vma=False,
    )
```

```python
import functools

import jax
import jax.numpy as jnp
from jax import lax
from jax.experimental import pallas as pl
from jax.experimental.pallas import tpu as pltpu
from jax.sharding import PartitionSpec as P

HIDDEN = -1e30
LOG2E = 1.4426950408889634
DOCS = 3
DOC_ROWS = 16
PIECES = 4
FAR = -1
TILE_HEADS = 2


def kernel(
    n,
    q_hbm,
    k_hbm,
    v_hbm,
    d_hbm,
    o_ref,
    q_ref,
    kv,
    docs,
    m_ref,
    acc_ref,
    qs,
    fill_sem,
    send_kv,
    recv_kv,
    recv_other,
    recv_far,
    recv_pair,
    send_far,
    ready_sem,
):
    rows, width = q_hbm.shape
    dim = k_hbm.shape[1]
    heads = width // dim
    levels = n // 4
    window = 3 * n // 4
    depth = (window + 3) // 4
    me = lax.axis_index("ctx")
    z = me // 4
    r = me % 4
    y = r // 2
    c = r % 2
    chip = me // 2
    up = me + 4
    across = z * 4 + (1 - y) * 2 + c
    partner = z * 4 + y * 2 + (1 - c)
    scale = dim ** (-0.5) * LOG2E
    top = z == levels - 1
    tail = top & (z >= depth)
    last = jnp.minimum(z, depth)
    quick = levels == 4
    source = (z == 1) & (y == 1) if quick else False
    aside = (z == 2) & (y == 0) if quick else False
    beyond = (z == 3) & (y == 1) if quick else False

    barrier = pltpu.get_barrier_semaphore()

    def greet(device):
        pl.semaphore_signal(
            barrier, inc=1, device_id={"ctx": device}, device_id_type=pl.DeviceIdType.MESH
        )

    @pl.when(z > 0)
    def _():
        greet(me - 4)

    @pl.when(z < levels - 1)
    def _():
        greet(up)

    greet(across)
    greet(partner)
    if quick:

        @pl.when(aside)
        def _():
            greet(me - 2)

        @pl.when(source)
        def _():
            greet(me + 8)

    assert rows <= 256 and rows % dim == 0
    stride = 2 * rows + DOC_ROWS
    half = rows // 2
    pieces = [(0, half), (half, half + DOC_ROWS), (rows + DOC_ROWS, half), (rows + DOC_ROWS + half, half)]

    def span(block, first=0, count=stride):
        return pl.ds(pl.multiple_of(block * stride + first, DOC_ROWS), count)

    doc_fill = pltpu.make_async_copy(d_hbm, docs, fill_sem.at[2])
    doc_fill.start()
    fills = [
        pltpu.make_async_copy(k_hbm, kv.at[span(me, 0, rows), :], fill_sem.at[0]),
        pltpu.make_async_copy(v_hbm, kv.at[span(me, rows + DOC_ROWS, rows), :], fill_sem.at[1]),
    ]
    for fill in fills:
        fill.start()
    query_fill = pltpu.make_async_copy(q_hbm, q_ref, fill_sem.at[3])
    query_fill.start()

    def landing(lands, level, piece, to_top):
        if lands > 1:
            return recv_pair.at[lands - 2, level]
        if lands == FAR:
            return recv_far.at[piece]
        if lands == 0:
            whole = (level == 0) & to_top if quick else False
            return recv_kv.at[level, jnp.where(whole, 0, piece or 0)]
        return recv_other.at[level, 0 if quick else piece]

    def copy_of(stream, lands, level, piece, block, device, to_top=False):
        place = span(block) if piece is None else span(block, *pieces[piece])
        return pltpu.make_async_remote_copy(
            src_ref=kv.at[place, :],
            dst_ref=kv.at[place, :],
            send_sem=send_kv.at[stream // 3, level] if stream < 4 else send_far.at[stream - 4],
            recv_sem=landing(lands, level, piece, to_top),
            device_id={"ctx": device},
            device_id_type=pl.DeviceIdType.MESH,
        )

    def start(stream, lands, level, piece, block, device):
        to_top = stream == 5 or (z == levels - 2 if stream == 0 else False)
        copy_of(stream, lands, level, piece, block, device, to_top).start()

    def arrived(lands, level, piece, block, device):
        copy_of(max(lands, 0), lands, level, piece, block, device, top).wait_recv()

    def sent(stream, level, block, device):
        copy_of(stream, 2, level, None, block, device).wait_send()

    def needs(some_chip, chunk):
        return (chunk <= some_chip) & (2 * chunk + 1 >= 2 * some_chip - window)

    def from_under(some_z, some_y, level):
        return (some_y == 0) & (some_z - level == depth) & needs(2 * some_z, 2 * level + 1)

    def spared(level):
        return (z == 2) & (y == 1) & (level == 0) if quick else False

    def climbs(level):
        return (z < levels - 1) & (z - level < depth) & jnp.logical_not(spared(level))

    def crosses(level):
        direct = needs(2 * z + 1 - y, 2 * level + y) & jnp.logical_not(from_under(z, 1 - y, level))
        return direct & jnp.logical_not(spared(level))

    def crossed(level):
        return needs(chip, 2 * level + 1 - y)

    def passes(level):
        return (z < levels - 1) & from_under(z + 1, y, level)

    def own(level):
        return level * 4 + r

    def other(level):
        return level * 4 + 2 * (1 - y) + c

    def relay(level, piece):
        @pl.when(climbs(level))
        def _():
            start(0, 0, level, piece, own(level), up)

        @pl.when(crosses(level))
        def _():
            start(1, 1, level, piece, own(level), across)

        if piece == len(pieces) - 1:
            start(2, 2, level, None, own(level), partner)

    def from_below(level):
        def plain():
            for piece in range(len(pieces)):
                arrived(0, level, piece, own(level), up)
                relay(level, piece)

        def whole():
            arrived(0, level, None, own(level), up)
            start(2, 2, level, None, own(level), partner)

        if not quick:
            plain()
            return
        ends = top & (level == 0)
        pl.when(ends)(whole)
        pl.when(jnp.logical_not(source | ends))(plain)

        @pl.when(source)
        def _():
            for piece in range(len(pieces)):
                arrived(0, level, piece, own(level), up)
                start(4, FAR, level, piece, own(level), me + 2)
                start(1, 1, level, piece, own(level), across)
            start(2, 2, level, None, own(level), partner)
            for piece in range(len(pieces)):
                start(0, 0, level, piece, own(level), up)
            pl.semaphore_wait(ready_sem, 1)
            for piece in range(len(pieces)):
                start(5, 0, level, piece, own(level), me + 8)

    def from_across(level):
        def piecewise(lands):
            for piece in range(len(pieces)):
                arrived(lands, level, piece, other(level), across)

                @pl.when(passes(level))
                def _():
                    start(4, 1, level, piece, other(level), up)

        @pl.when(crossed(level))
        def _():
            if quick:
                pl.when(passes(level))(lambda: piecewise(FAR))
                pl.when(jnp.logical_not(passes(level)))(
                    lambda: arrived(1, level, None, other(level), across)
                )
            else:
                piecewise(1)
            start(3, 3, level, None, other(level), partner)

    def own_pair(level):
        arrived(2, level, None, level * 4 + 2 * y + 1 - c, partner)

    def other_pair(level):
        @pl.when(crossed(level))
        def _():
            arrived(3, level, None, level * 4 + 2 * (1 - y) + 1 - c, partner)

    def finish(level):
        copies = 1 + jnp.where(climbs(level), 1, 0) + jnp.where(crosses(level), 1, 0)
        for many in range(1, 4):

            @pl.when(copies == many)
            def _():
                everything = kv.at[pl.ds(0, many * stride), :]
                pltpu.make_async_remote_copy(
                    src_ref=everything,
                    dst_ref=everything,
                    send_sem=send_kv.at[0, level],
                    recv_sem=recv_pair.at[0, level],
                    device_id={"ctx": partner},
                    device_id_type=pl.DeviceIdType.MESH,
                ).wait_send()

        if quick:

            @pl.when(source & (level == 0))
            def _():
                sent(4, level, own(level), me + 2)
                sent(5, level, own(level), me + 8)

        @pl.when(crossed(level))
        def _():
            sent(3, level, other(level), partner)

            @pl.when(passes(level))
            def _():
                sent(4, level, other(level), up)

    doc_fill.wait()
    ids = docs[...]
    bounds = [jnp.sum(jnp.where(ids < doc, 1.0, 0.0), keepdims=True) for doc in range(1, DOCS)]
    bounds = [jnp.broadcast_to(bound, (1, dim)) for bound in bounds]
    bounds.append(jnp.zeros((DOC_ROWS - len(bounds), dim), jnp.float32))
    kv[span(me, rows, DOC_ROWS), :] = jnp.concatenate(bounds, axis=0).astype(jnp.bfloat16)
    greeters = 2 + jnp.minimum(z, 1) + jnp.minimum(levels - 1 - z, 1)
    if quick:
        greeters = greeters + jnp.where(source | beyond, 1, 0)
    pl.semaphore_wait(barrier, greeters)
    if quick:

        @pl.when(beyond)
        def _():
            pl.semaphore_signal(
                ready_sem, inc=1, device_id={"ctx": me - 8}, device_id_type=pl.DeviceIdType.MESH
            )

    fills[0].wait()
    for piece in range(len(pieces)):
        if pieces[piece][0] == rows + DOC_ROWS:
            fills[1].wait()
        relay(z, piece)

    lane = lax.broadcasted_iota(jnp.int32, (rows, dim), 1)
    row = lax.broadcasted_iota(jnp.int32, (rows, dim), 0).astype(jnp.float32)

    def doc_of(block):
        bounds = kv[span(block, rows, DOC_ROWS), :].astype(jnp.float32)
        number = jnp.zeros((rows, dim), jnp.int32)
        for doc in range(1, DOCS):
            number = number + jnp.where(row >= bounds[doc - 1 : doc, :], 1, 0)
        return number

    query_marks = jnp.where(lane == doc_of(me), 0.0, HIDDEN).astype(jnp.bfloat16)
    query_fill.wait()
    for head in range(heads):
        here = slice(head * rows, (head + 1) * rows)
        qs[here, :dim] = q_ref[:, head * dim : (head + 1) * dim]
        qs[here, dim:] = query_marks

    tile_rows = TILE_HEADS * rows
    tiles = heads // TILE_HEADS

    def attend(blocks, first=False):
        ks, vs = [], []
        for block in blocks:
            marks = jnp.where(lane == doc_of(block), 1.0, 0.0).astype(jnp.bfloat16)
            ks.append(jnp.concatenate([kv[span(block, 0, rows), :], marks], axis=1))
            vs.append(jnp.concatenate([kv[span(block, rows + DOC_ROWS, rows), :], jnp.ones((rows, dim), jnp.bfloat16)], axis=1))
        k_block = jnp.concatenate(ks, axis=0)
        v_block = jnp.concatenate(vs, axis=0)
        length = k_block.shape[0]

        def scores(tile):
            return lax.dot_general(
                qs[tile * tile_rows : (tile + 1) * tile_rows, :],
                k_block,
                (((1,), (1,)), ((), ())),
                preferred_element_type=jnp.float32,
            )

        following = scores(0)
        for tile in range(tiles):
            s = following
            if tile + 1 < tiles:
                following = scores(tile + 1)
            here = slice(tile * tile_rows, (tile + 1) * tile_rows)
            if first:
                key_id = lax.broadcasted_iota(jnp.int32, (rows, rows), 1)
                query_id = lax.broadcasted_iota(jnp.int32, (rows, rows), 0)
                hide = jnp.where(key_id <= query_id, 0.0, HIDDEN)
                s = s + jnp.concatenate([hide] * TILE_HEADS, axis=0)
            new = jnp.broadcast_to(jnp.max(s, axis=1, keepdims=True), (tile_rows, dim))
            if not first:
                old = m_ref[here]
                new = jnp.maximum(old, new)
            m_ref[here] = new
            w = jnp.exp2((s - jnp.tile(new, (1, length // dim))) * scale)
            part = jnp.dot(w.astype(jnp.bfloat16), v_block, preferred_element_type=jnp.float32)
            if first:
                acc_ref[here] = part
            else:
                acc_ref[here] = (
                    acc_ref[here] * jnp.tile(jnp.exp2((old - new) * scale), (1, 2)) + part
                )

    attend([me], True)
    own_pair(z)

    @pl.when(c == 1)
    def _():
        attend([me - 1])

    def early(level):
        return jnp.logical_not(top) & (climbs(level) | crosses(level))

    def ahead(i, carry):
        pl.when(early(z - i))(lambda: from_below(z - i))
        return carry

    lax.fori_loop(1, last + 1, ahead, 0)

    def pair_of(level):
        return level * 4 + 2 * y + 1 - c

    def other_pair_of(level):
        return level * 4 + 2 * (1 - y) + 1 - c

    for i in range(1, depth + 1):

        @pl.when(z >= i)
        def _():
            level = z - i
            final = (z == i) | (i == depth)
            late = final & (y == 1)
            pairs = late & jnp.logical_not(tail)
            before = jnp.logical_not(pairs)
            both = before & crossed(level + 1)
            hooked = top & (y == 1) if i > 1 else False
            waits = jnp.logical_not(early(level))

            closing = late & tail
            pl.when(before & waits & jnp.logical_not(hooked | closing))(lambda: from_below(level))
            far = final & jnp.logical_not(top) & (y == 0)
            pl.when(far)(lambda: from_across(level))
            from_across(level + 1)
            pl.when(closing)(lambda: from_below(level))
            pl.when(pairs)(lambda: from_across(level))
            pl.when(pairs)(lambda: other_pair(level + 1))

            @pl.when(both | pairs)
            def _():
                attend(
                    [
                        jnp.where(both, own(level), other(level + 1)),
                        jnp.where(both, other(level + 1), other_pair_of(level + 1)),
                    ]
                )

            if i + 1 < depth:
                last_but = z == i + 1
                pl.when(top & (y == 1) & jnp.logical_not(final | last_but))(
                    lambda: from_below(level - 1)
                )

            pl.when(final & tail)(lambda: from_across(level))
            pl.when(pairs & waits)(lambda: from_below(level))

            @pl.when(before | crossed(level))
            def _():
                pl.when(before)(lambda: own_pair(level))
                pl.when(both)(lambda: other_pair(level + 1))
                pl.when(pairs)(lambda: other_pair(level))
                attend(
                    [
                        jnp.where(both, pair_of(level), jnp.where(pairs, other(level), own(level))),
                        jnp.where(
                            both,
                            other_pair_of(level + 1),
                            jnp.where(pairs, other_pair_of(level), pair_of(level)),
                        ),
                    ]
                )

    level = z - last
    pairs = (y == 1) & (z > 0) & jnp.logical_not(tail)
    pl.when((z == 0) | (top & jnp.logical_not(tail) & (y == 0)))(lambda: from_across(level))

    pl.when(pairs)(lambda: own_pair(level))
    pl.when(jnp.logical_not(pairs))(lambda: other_pair(level))

    @pl.when(pairs | crossed(level))
    def _():
        attend(
            [
                jnp.where(pairs, own(level), other(level)),
                jnp.where(pairs, pair_of(level), other_pair_of(level)),
            ]
        )

    for head in range(heads):
        here = slice(head * rows, (head + 1) * rows)
        o_ref[:, head * dim : (head + 1) * dim] = (acc_ref[here, :dim] / acc_ref[here, dim:]).astype(
            o_ref.dtype
        )

    def drain(i, carry):
        finish(z - i)
        return carry

    lax.fori_loop(0, last + 1, drain, 0)


def solution(mesh):
    n = mesh.shape["ctx"]

    def on_device(queries, keys, values, doc_ids):
        rows, width = queries.shape
        dim = keys.shape[1]
        heads = width // dim
        levels = n // 4
        anywhere = pl.BlockSpec(memory_space=pl.ANY)
        return pl.pallas_call(
            functools.partial(kernel, n),
            out_shape=jax.ShapeDtypeStruct((rows, width), jnp.bfloat16),
            in_specs=[anywhere] * 4,
            out_specs=pl.BlockSpec(memory_space=pltpu.VMEM),
            scratch_shapes=[
                pltpu.VMEM((rows, width), jnp.bfloat16),
                pltpu.VMEM((n * (2 * rows + DOC_ROWS), dim), jnp.bfloat16),
                pltpu.VMEM((rows // dim, dim), jnp.int32),
                pltpu.VMEM((heads * rows, dim), jnp.float32),
                pltpu.VMEM((heads * rows, 2 * dim), jnp.float32),
                pltpu.VMEM((heads * rows, 2 * dim), jnp.bfloat16),
                pltpu.SemaphoreType.DMA((4,)),
                pltpu.SemaphoreType.DMA((2, levels)),
                pltpu.SemaphoreType.DMA((max(levels - 1, 1), PIECES)),
                pltpu.SemaphoreType.DMA((levels, 1 if levels == 4 else PIECES)),
                pltpu.SemaphoreType.DMA((PIECES,)),
                pltpu.SemaphoreType.DMA((2, levels)),
                pltpu.SemaphoreType.DMA((2,)),
                pltpu.SemaphoreType.REGULAR,
            ],
            compiler_params=pltpu.CompilerParams(collective_id=0, has_side_effects=True, vmem_limit_bytes=16 * 1024 * 1024),
        )(*[pltpu.with_memory_space_constraint(a, pltpu.HBM) for a in (queries, keys, values, doc_ids.reshape(rows // dim, dim))])

    spec = P(("groups", "ctx"), None)
    return jax.shard_map(
        on_device,
        mesh=mesh,
        in_specs=(spec, spec, spec, P(("groups", "ctx"))),
        out_specs=spec,
        check_vma=False,
    )
```
